256 devices in a mesh: region: 32 (over z, y), angle: 8 (over x, core).
Axes of the slice: x: 4, y: 4, z: 8, core: 2. Of those that a mesh axis runs over, the one named last changes fastest.
Arguments:
- volume: float32 [512, 128, 128], P('region'), may hold values from -6 to 6
- blocks: bfloat16 [65536, 128, 128], P(('region', 'angle')), may hold values from -0.1875 to 0.1875
- tile_of: int32 [65536], P(('region', 'angle')), may hold values from 0 to 15
- slot_of: int32 [65536], P(('region', 'angle')), may hold values from 0 to 31
- live_count: int32 [256], P(('region', 'angle')), may hold values from 96 to 256, as said below
- ray_of: int32 [8192], P(('region', 'angle')), may hold values from 0 to 7
- sinogram: float32 [2048, 128, 128], P(('region', 'angle')), may hold values from -6 to 6
- ray_weight: float32 [2048, 128], P(('region', 'angle')), may hold values from 0.5 to 2
- pixel_weight: float32 [512, 128], P('region'), may hold values from 0.1 to 0.5
Outputs:
- updated: float32 [512, 128, 128], P(('region', 'angle'))
- residual: float32 [2048, 128, 128], P(('region', 'angle'))
The draws below stay inside these ranges and needn't reach their ends.
Inputs may be any that keep to these rules, and one draw needn't show every extreme that they name: Blocks at positions 256 * d + j with j < live_count[d] are in use, the others are ignored; every device uses at least 96 blocks, and some device uses all 256.
All inputs are finite; a program needn't handle non-finite values.
Results may differ from the reference program's by a relative error of at most 0.0039.
Values may be sent and summed in bfloat16 or wider, within the bound.
A program may use at most 128 MiB of HBM per device.

```python
import math
import jax
import jax.numpy as jnp
from jax import lax

BLK = 128
SLICES = 128
TILE_DEV = 16
RAY_DEV = 8
CAP = 1
NNZ_DEV = 256
TILES = 512
RAYS = 2048
ENTRIES = 65536
SLOTS = 32
MAPS = 8192
N_REGION = 32
N_ANGLE = 8
DEVICES = 256


def draw_live_count(key, part):
    key_counts, key_fullest = jax.random.split(jax.random.fold_in(key, 7))
    counts = jax.random.randint(key_counts, (DEVICES,), 3 * NNZ_DEV // 8, NNZ_DEV + 1)
    fullest = jax.random.randint(key_fullest, (), 0, DEVICES)
    return jnp.where(jnp.arange(DEVICES) == fullest, NNZ_DEV, counts).astype(jnp.int32)


def touch_ends(entries, key, smallest, high):
    spot = [jax.random.randint(jax.random.fold_in(key, axis), (), 0, length) for axis, length in enumerate(entries.shape)]
    longest = entries.shape.index(max(entries.shape))
    neighbour = spot[:longest] + [(spot[longest] + 1) % entries.shape[longest]] + spot[longest + 1:]
    return entries.at[tuple(spot)].set(smallest).at[tuple(neighbour)].set(high)


def block_levels(key, extent, cuts, least, largest):
    factor_of, own = 1.0, jax.random.fold_in(key, 6)
    for dim, shards_of in cuts:
        draws = jnp.exp(jax.random.uniform(jax.random.fold_in(own, dim), (shards_of,), jnp.float32, least / len(cuts), largest / len(cuts)))
        factor_of = factor_of * jnp.repeat(draws, extent[dim] // shards_of).reshape([-1 if axis == dim else 1 for axis in range(len(extent))])
    return factor_of


def centred(rng, dims, deviation, limit, shards=(), held_as=jnp.bfloat16):
    drawn = deviation * jax.random.normal(rng, dims, jnp.float32)
    if shards:
        drawn = drawn * block_levels(rng, dims, shards, -0.22, 0.18)
    return jnp.clip(drawn, -limit, limit).astype(held_as)


def setup_inputs(seed: int = 0) -> dict:
    arg_keys = jax.random.split(jax.random.key(seed), 10)
    volume = centred(arg_keys[0], (TILES, SLICES, BLK), 1.0, 6.0, ((0, 32),), jnp.float32)
    blocks = centred(arg_keys[1], (ENTRIES, BLK, BLK), (BLK * 8) ** -0.5, 0.1875, ((0, 256),))
    tile_of = touch_ends(jax.random.randint(arg_keys[2], (ENTRIES,), 0, TILE_DEV), jax.random.fold_in(arg_keys[2], 1), 0, TILE_DEV - 1).astype(jnp.int32)
    slot_of = touch_ends(jax.random.randint(arg_keys[3], (ENTRIES,), 0, SLOTS), jax.random.fold_in(arg_keys[3], 1), 0, SLOTS - 1).astype(jnp.int32)
    live_count = draw_live_count(jax.random.fold_in(arg_keys[9], 71), 0)
    ray_of = touch_ends(jax.random.randint(arg_keys[5], (MAPS,), 0, RAY_DEV), jax.random.fold_in(arg_keys[5], 1), 0, RAY_DEV - 1).astype(jnp.int32)
    sinogram = centred(arg_keys[6], (RAYS, SLICES, BLK), 1.0, 6.0, ((0, 256),), jnp.float32)
    ray_weight = jnp.clip(jnp.exp(math.log(2.0) - 1.3862944 * jax.random.uniform(arg_keys[7], (RAYS, BLK), jnp.float32) ** block_levels(arg_keys[7], (RAYS, BLK), ((0, 256),), -0.2, 0.2)), 0.5, 2.0)
    pixel_weight = jnp.clip(jnp.exp(math.log(0.5) - 1.609438 * jax.random.uniform(arg_keys[8], (TILES, BLK), jnp.float32) ** block_levels(arg_keys[8], (TILES, BLK), ((0, 32),), -0.2, 0.2)), 0.1, 0.5)
    return {"volume": volume, "blocks": blocks, "tile_of": tile_of, "slot_of": slot_of, "live_count": live_count, "ray_of": ray_of, "sinogram": sinogram, "ray_weight": ray_weight, "pixel_weight": pixel_weight}


def reference(volume, blocks, tile_of, slot_of, live_count, ray_of, sinogram, ray_weight, pixel_weight):
    device_ids = jnp.arange(DEVICES, dtype=jnp.int32)
    region_idx = device_ids // N_ANGLE
    angle_idx = device_ids % N_ANGLE
    slot_ids = slot_of.reshape(DEVICES, NNZ_DEV)
    owner_idx = slot_ids // CAP
    target_dev = owner_idx * N_ANGLE + angle_idx[:, None]
    map_index = target_dev * (N_REGION * CAP) + region_idx[:, None] * CAP + slot_ids % CAP
    ray_index = (target_dev * RAY_DEV + ray_of[map_index]).astype(jnp.int32)
    tile_index = (region_idx[:, None] * TILE_DEV + tile_of.reshape(DEVICES, NNZ_DEV)).astype(jnp.int32)
    live_mask = jnp.arange(NNZ_DEV, dtype=jnp.int32)[None, :] < live_count[:, None]
    volume_b = volume.astype(jnp.bfloat16)
    block_sets = blocks.reshape(DEVICES, NNZ_DEV, BLK, BLK)

    def forward(total, inputs):
        block_set, tile_ids, ray_ids, is_live = inputs
        picked = volume_b[tile_ids].astype(jnp.float32)
        product = jnp.einsum("esp,erp->esr", picked, block_set.astype(jnp.float32), precision=lax.Precision.HIGHEST)
        product = jnp.where(is_live[:, None, None], product, jnp.zeros_like(product))
        return total.at[ray_ids].add(product), None

    projection, _ = lax.scan(forward, jnp.zeros((RAYS, SLICES, BLK), jnp.float32), (block_sets, tile_index, ray_index, live_mask))
    residual = ray_weight[:, None, :] * (sinogram - projection)
    residual_b = residual.astype(jnp.bfloat16)

    def backward(total, inputs):
        block_set, tile_ids, ray_ids, is_live = inputs
        slot_rows = residual_b[ray_ids].astype(jnp.float32)
        product = jnp.einsum("esr,erp->esp", slot_rows, block_set.astype(jnp.float32), precision=lax.Precision.HIGHEST)
        product = jnp.where(is_live[:, None, None], product, jnp.zeros_like(product))
        return total.at[tile_ids].add(product), None

    gradient, _ = lax.scan(backward, jnp.zeros((TILES, SLICES, BLK), jnp.float32), (block_sets, tile_index, ray_index, live_mask))
    updated = volume + pixel_weight[:, None, :] * gradient
    return updated, residual
```

```python
import functools

import jax
import jax.numpy as jnp
from jax import lax
from jax.experimental import pallas as pl
from jax.experimental.pallas import tpu as pltpu
from jax.sharding import PartitionSpec as P

MESH = pl.DeviceIdType.MESH
BF = jnp.bfloat16
F32 = jnp.float32
I32 = jnp.int32

CHUNKS = 2
UNROLL = 8
NY = 4


def iota(shape, dim):
    return lax.broadcasted_iota(I32, shape, dim)


def order(key_row, live_row, payload_row, pad, keys, group, places):
    n = key_row.shape[1]
    row, col = iota((n, n), 0), iota((n, n), 1)
    key_row = jnp.where(live_row, key_row, keys)
    diag = row == col
    key_col = jnp.sum(jnp.where(diag, key_row, 0), axis=1, keepdims=True)
    payload_col = jnp.sum(jnp.where(diag, payload_row, 0), axis=1, keepdims=True)
    earlier = jnp.where((key_col == key_row) & (col < row), 1, 0)
    rank_col = jnp.sum(earlier, axis=1, keepdims=True)
    lane = iota((n, 128), 1)
    same = key_col == lane
    count_row = jnp.sum(jnp.where(same, 1, 0), axis=0, keepdims=True)
    run_row = (count_row + (group - 1)) & -group
    start_col = jnp.sum(jnp.where(lane < key_col, run_row, 0), axis=1, keepdims=True)
    place_col = jnp.where(key_col < keys, start_col + rank_col, 1 << 20)
    hit = place_col == iota((n, places), 1)
    entry = iota((n, places), 0)
    src = jnp.sum(jnp.where(hit, entry, 0), axis=0, keepdims=True)
    payload = jnp.sum(jnp.where(hit, payload_col - pad, 0), axis=0, keepdims=True) + pad
    opens = jnp.sum(jnp.where(hit & (rank_col == 0), 1, 0), axis=0, keepdims=True)
    last = jnp.max(jnp.where(same, place_col, -1), axis=0, keepdims=True)
    return src, payload, opens, last


def kernel(
    n_region, n_angle, chunks,
    count_s, ray_s, tile_v, slot_v, ray_v, rw_v, pw_v, volume_h, blocks_h, sino_h,
    updated_h, residual_h,
    blocks, vol, sino, vol_b, runs_f, runs_b, runs_p, rows_v, rows_s,
    send1, recv1, res, res_b, send2, recv2, grad, send3, recv3, upd,
    sem_in, sem_rows, sem_out, ssem1, rsem1, ssem2, rsem2, ssem3, rsem3,
):
    r = lax.axis_index("region")
    a = lax.axis_index("angle")
    z, y = r // NY, lax.rem(r, NY)
    nz = n_region // NY
    entries = blocks.shape[0]
    tiles = vol.shape[0]
    slots = n_region
    rays = sino.shape[0]
    size = vol.shape[1]
    m = size // chunks
    pairs_f = runs_f.shape[0] - 1
    pairs_b = runs_b.shape[0] - 1
    share = tiles // n_angle

    load_b = pltpu.make_async_copy(blocks_h, blocks, sem_in.at[0])
    load_v = pltpu.make_async_copy(volume_h, vol, sem_in.at[1])
    load_s = pltpu.make_async_copy(sino_h, sino, sem_in.at[2])
    load_v.start()
    load_b.start()
    load_s.start()

    far = lambda d, n: min(d, n - d)
    steps = [(dz, dy) for dz in range(nz) for dy in range(NY) if (dz, dy) != (0, 0)]
    steps.sort(key=lambda o: -(far(o[0], nz) + far(o[1], NY)))
    peers = [lax.rem(z + dz, nz) * NY + lax.rem(y + dy, NY) for dz, dy in steps]
    others = [lax.rem(a + k, n_angle) for k in range(1, n_angle)]
    barrier = pltpu.get_barrier_semaphore()
    for peer in peers:
        pl.semaphore_signal(barrier, inc=1, device_id=(peer, a), device_id_type=MESH)
    for other in others:
        pl.semaphore_signal(barrier, inc=1, device_id=(r, other), device_id_type=MESH)

    live = lax.broadcasted_iota(I32, (1, entries), 1) < count_s[0]
    tile_row, slot_row, ray_row = tile_v[...], slot_v[...], ray_v[...]
    places = rows_v.shape[1]
    every = lax.broadcasted_iota(I32, ray_row.shape, 1) < n_region
    empty = lambda last, group, none: jnp.where(last < 0, none, last >> (group - 1))
    pad = lambda x: jnp.concatenate([x, jnp.zeros((1, places - x.shape[1]), I32)], axis=1)
    src, payload, opens, last = order(slot_row, live, tile_row, tiles, slots, 2, places)
    rows = [src, payload, opens, pad(empty(last, 2, pairs_f))]
    src, payload, opens, last = order(tile_row, live, slot_row, slots, tiles, 2, places)
    rows += [src, payload, opens, pad(empty(last, 2, pairs_b))]
    src, _, opens, last = order(ray_row, every, ray_row, 0, rays, 1, 128)
    rows += [pad(src), pad(opens), pad(empty(last, 1, n_region))]
    for i, row in enumerate(rows):
        rows_v[i : i + 1, :] = row
    to_scalar = pltpu.make_async_copy(rows_v, rows_s, sem_rows)
    to_scalar.start()

    load_v.wait()
    for t in range(tiles):
        vol_b[t] = vol[t].astype(BF)
    vol_b[tiles] = jnp.zeros((size, size), BF)
    for c in range(chunks):
        recv2[c][slots] = jnp.zeros((m, size), BF)
    runs_f[pairs_f] = jnp.zeros((m, size), BF)
    runs_b[pairs_b] = jnp.zeros((m, size), F32)
    runs_p[n_region] = jnp.zeros((m, size), F32)
    to_scalar.wait()
    load_b.wait()

    def products(left, base, transposed, runs, pairs):
        def step(g, total):
            for u in range(UNROLL):
                p = g * UNROLL + u
                e0, e1 = rows_s[base, 2 * p], rows_s[base, 2 * p + 1]
                k0, k1 = rows_s[base + 1, 2 * p], rows_s[base + 1, 2 * p + 1]
                opened = rows_s[base + 2, 2 * p]
                lhs = jnp.concatenate([left[k0], left[k1]], axis=1)
                rhs = jnp.concatenate([blocks[e0], blocks[e1]], axis=1 if transposed else 0)
                dims = (((1,), (1,)), ((), ())) if transposed else (((1,), (0,)), ((), ()))
                product = lax.dot_general(lhs, rhs, dims, preferred_element_type=F32)
                total = jnp.where(opened > 0, 0.0, total) + product
                runs[p] = total.astype(runs.dtype)
            return total

        lax.fori_loop(0, pairs // UNROLL, step, jnp.zeros((m, size), F32))

    def exchange(src, dst, ssem, rsem, c):
        rows_at = pl.ds(c * m, m)
        for peer in peers:
            pltpu.make_async_remote_copy(
                src_ref=src.at[peer, rows_at], dst_ref=dst[c].at[r],
                send_sem=ssem.at[c], recv_sem=rsem.at[c], device_id=(peer, a), device_id_type=MESH,
            ).start()
        dst[c][r] = src[r, rows_at, :]

    def arrived(dst, sem, c):
        part = dst[c].at[pl.ds(0, n_region - 1)]
        pltpu.make_async_copy(part, part, sem.at[c]).wait()

    for c in range(chunks):
        rows_at = pl.ds(c * m, m)
        products(vol_b.at[:, rows_at], 0, True, runs_f, pairs_f)
        for s in range(slots):
            send1[s, rows_at, :] = runs_f[rows_s[3, s]]
        if c == 0:
            pl.semaphore_wait(barrier, len(peers) + len(others))
        exchange(send1, recv1, ssem1, rsem1, c)

    load_s.wait()
    for c in range(chunks):
        rows_at = pl.ds(c * m, m)
        arrived(recv1, rsem1, c)
        total = jnp.zeros((m, size), F32)
        for k in range(n_region):
            total = jnp.where(rows_s[9, k] > 0, 0.0, total) + recv1[c][rows_s[8, k]].astype(F32)
            runs_p[k] = total
        for j in range(rays):
            value = rw_v[j : j + 1, :] * (sino[j, rows_at, :] - runs_p[rows_s[10, j]])
            res[j, rows_at, :] = value
            res_b[j, rows_at, :] = value.astype(BF)
        for s in range(n_region):
            send2[s, rows_at, :] = res_b[ray_s[s], rows_at, :]
        exchange(send2, recv2, ssem2, rsem2, c)
    out_r = pltpu.make_async_copy(res, residual_h, sem_out.at[0])
    out_r.start()

    for c in range(chunks):
        rows_at = pl.ds(c * m, m)
        arrived(recv2, rsem2, c)
        products(recv2[c], 4, False, runs_b, pairs_b)
        for t in range(tiles):
            value = runs_b[rows_s[7, t]]
            grad[t, rows_at, :] = value
            send3[t // share, c, t % share] = value.astype(BF)
        for other in others:
            pltpu.make_async_remote_copy(
                src_ref=send3.at[other, c], dst_ref=recv3.at[a, c],
                send_sem=ssem3.at[c], recv_sem=rsem3.at[c], device_id=(r, other), device_id_type=MESH,
            ).start()
        recv3[a, c] = jnp.zeros((share, m, size), BF)

    for c in range(chunks):
        rows_at = pl.ds(c * m, m)
        part = recv3.at[pl.ds(0, n_angle - 1), c]
        pltpu.make_async_copy(part, part, rsem3.at[c]).wait()
        for t in range(share):
            mine = a * share + t
            total = grad[mine, rows_at, :]
            for k in range(n_angle):
                total = total + recv3[k, c, t].astype(F32)
            upd[t, rows_at, :] = vol[mine, rows_at, :] + pw_v[pl.ds(mine, 1), :] * total
    out_u = pltpu.make_async_copy(upd, updated_h, sem_out.at[1])
    out_u.start()

    for c in range(chunks):
        for src, sem in ((send1, ssem1), (send2, ssem2)):
            part = src.at[pl.ds(0, n_region - 1), pl.ds(c * m, m)]
            pltpu.make_async_copy(part, part, sem.at[c]).wait()
        part = send3.at[pl.ds(0, n_angle - 1), c]
        pltpu.make_async_copy(part, part, ssem3.at[c]).wait()
    out_r.wait()
    out_u.wait()


def up(value, step):
    return -(-value // step) * step


def body(volume, blocks, tile_of, slot_of, live_count, ray_of, sinogram, ray_weight, pixel_weight):
    n_region = lax.axis_size("region")
    n_angle = lax.axis_size("angle")
    entries, size, _ = blocks.shape
    tiles, rays = volume.shape[0], sinogram.shape[0]
    chunks = CHUNKS
    m = size // chunks
    share = tiles // n_angle
    pairs_f = up((entries + n_region) // 2, UNROLL)
    pairs_b = up((entries + tiles) // 2, UNROLL)
    places = up(2 * max(pairs_f, pairs_b), 128)
    ray_row = jnp.pad(ray_of, (0, 128 - n_region)).reshape(1, 128)
    smem = pl.BlockSpec(memory_space=pltpu.SMEM)
    vmem = pl.BlockSpec(memory_space=pltpu.VMEM)
    hbm = pl.BlockSpec(memory_space=pl.ANY)
    return pl.pallas_call(
        functools.partial(kernel, n_region, n_angle, chunks),
        out_shape=(
            jax.ShapeDtypeStruct((share, size, size), F32),
            jax.ShapeDtypeStruct((rays, size, size), F32),
        ),
        in_specs=[smem, smem, vmem, vmem, vmem, vmem, vmem, hbm, hbm, hbm],
        out_specs=(hbm, hbm),
        scratch_shapes=[
            pltpu.VMEM((entries, size, size), BF),
            pltpu.VMEM((tiles, size, size), F32),
            pltpu.VMEM((rays, size, size), F32),
            pltpu.VMEM((tiles + 1, size, size), BF),
            pltpu.VMEM((pairs_f + 1, m, size), BF),
            pltpu.VMEM((pairs_b + 1, m, size), F32),
            pltpu.VMEM((n_region + 1, m, size), F32),
            pltpu.VMEM((16, places), I32),
            pltpu.SMEM((16, places), I32),
            pltpu.VMEM((n_region, size, size), BF),
            [pltpu.VMEM((n_region, m, size), BF)] * chunks,
            pltpu.VMEM((rays, size, size), F32),
            pltpu.VMEM((rays, size, size), BF),
            pltpu.VMEM((n_region, size, size), BF),
            [pltpu.VMEM((n_region + 1, m, size), BF)] * chunks,
            pltpu.VMEM((tiles, size, size), F32),
            pltpu.VMEM((n_angle, chunks, share, m, size), BF),
            pltpu.VMEM((n_angle, chunks, share, m, size), BF),
            pltpu.VMEM((share, size, size), F32),
            pltpu.SemaphoreType.DMA((3,)),
            pltpu.SemaphoreType.DMA,
            pltpu.SemaphoreType.DMA((2,)),
        ]
        + [pltpu.SemaphoreType.DMA((chunks,))] * 6,
        compiler_params=pltpu.CompilerParams(
            collective_id=0, has_side_effects=True, vmem_limit_bytes=56 * 2**20
        ),
    )(
        live_count, ray_of, tile_of.reshape(1, entries), slot_of.reshape(1, entries), ray_row,
        ray_weight, pixel_weight, volume, blocks, sinogram,
    )


def solution(mesh):
    placed = (
        P("region", None, None),
        P(("region", "angle"), None, None),
        P(("region", "angle")),
        P(("region", "angle")),
        P(("region", "angle")),
        P(("region", "angle")),
        P(("region", "angle"), None, None),
        P(("region", "angle"), None),
        P("region", None),
    )
    return jax.shard_map(
        body,
        mesh=mesh,
        in_specs=placed,
        out_specs=(P(("region", "angle"), None, None), P(("region", "angle"), None, None)),
        check_vma=False,
    )
```

```python
import functools

import jax
import jax.numpy as jnp
from jax import lax
from jax.experimental import pallas as pl
from jax.experimental.pallas import tpu as pltpu
from jax.sharding import PartitionSpec as P

MESH = pl.DeviceIdType.MESH
BF = jnp.bfloat16
F32 = jnp.float32
I32 = jnp.int32

SIZES = (48, 48, 32)
UNROLL_F, UNROLL_B = 18, 17
LOADS = 4
NY = 4


def iota(shape, dim):
    return lax.broadcasted_iota(I32, shape, dim)


def order(key_row, live_row, payload_row, pad, keys, group, places):
    n = key_row.shape[1]
    row, col = iota((n, n), 0), iota((n, n), 1)
    key_row = jnp.where(live_row, key_row, keys)
    diag = row == col
    key_col = jnp.sum(jnp.where(diag, key_row, 0), axis=1, keepdims=True)
    payload_col = jnp.sum(jnp.where(diag, payload_row, 0), axis=1, keepdims=True)
    earlier = jnp.where((key_col == key_row) & (col < row), 1, 0)
    rank_col = jnp.sum(earlier, axis=1, keepdims=True)
    lane = iota((n, 128), 1)
    same = key_col == lane
    count_row = jnp.sum(jnp.where(same, 1, 0), axis=0, keepdims=True)
    run_row = (count_row + (group - 1)) & -group
    start_col = jnp.sum(jnp.where(lane < key_col, run_row, 0), axis=1, keepdims=True)
    place_col = jnp.where(key_col < keys, start_col + rank_col, 1 << 20)
    hit = place_col == iota((n, places), 1)
    entry = iota((n, places), 0)
    src = jnp.sum(jnp.where(hit, entry, 0), axis=0, keepdims=True)
    payload = jnp.sum(jnp.where(hit, payload_col - pad, 0), axis=0, keepdims=True) + pad
    opens = jnp.sum(jnp.where(hit & (rank_col == 0), 1, 0), axis=0, keepdims=True)
    last = jnp.max(jnp.where(same, place_col, -1), axis=0, keepdims=True)
    return src, payload, opens, last


def kernel(
    n_region, n_angle, sizes,
    count_s, ray_s, tile_v, slot_v, ray_v, rw_v, pw_v, volume_h, blocks_h, sino_h,
    upd, res,
    blocks, vol, sino, vol_b, runs_f, runs_b, runs_p, rows_v, rows_s,
    send1, recv1, res_b, send2, recv2, grad, send3, recv3,
    sem_in, sem_rows, ssem1, rsem1, ssem2, rsem2, ssem3, rsem3,
):
    r = lax.axis_index("region")
    a = lax.axis_index("angle")
    z, y = r // NY, lax.rem(r, NY)
    nz = n_region // NY
    entries = blocks.shape[0]
    tiles = vol.shape[0]
    slots = n_region
    rays = sino.shape[0]
    size = vol.shape[1]
    chunks = len(sizes)
    parts = [pl.ds(sum(sizes[:c]), m) for c, m in enumerate(sizes)]
    most = max(sizes)
    pairs_f = runs_f.shape[0] - 1
    pairs_b = runs_b.shape[0] - 1
    share = tiles // n_angle

    piece = entries // LOADS
    load_b = [
        pltpu.make_async_copy(blocks_h.at[pl.ds(i * piece, piece)], blocks.at[pl.ds(i * piece, piece)], sem_in.at[2 + i])
        for i in range(LOADS)
    ]
    load_v = pltpu.make_async_copy(volume_h, vol, sem_in.at[0])
    load_s = pltpu.make_async_copy(sino_h, sino, sem_in.at[1])
    load_v.start()
    for load in load_b:
        load.start()
    load_s.start()

    far = lambda d, n: min(d, n - d)
    steps = [(dz, dy) for dz in range(nz) for dy in range(NY) if (dz, dy) != (0, 0)]
    steps.sort(key=lambda o: -(far(o[0], nz) + far(o[1], NY)))
    peers = [lax.rem(z + dz, nz) * NY + lax.rem(y + dy, NY) for dz, dy in steps]
    others = [lax.rem(a + k, n_angle) for k in range(1, n_angle)]
    barrier = pltpu.get_barrier_semaphore()
    for peer in peers:
        pl.semaphore_signal(barrier, inc=1, device_id=(peer, a), device_id_type=MESH)
    for other in others:
        pl.semaphore_signal(barrier, inc=1, device_id=(r, other), device_id_type=MESH)

    live = lax.broadcasted_iota(I32, (1, entries), 1) < count_s[0]
    tile_row, slot_row = tile_v[...], slot_v[...]
    ray_row = jnp.concatenate([ray_v[...], jnp.zeros((1, 128 - n_region), I32)], axis=1)
    places = rows_v.shape[1]
    every = lax.broadcasted_iota(I32, ray_row.shape, 1) < n_region
    empty = lambda last, group, none: jnp.where(last < 0, none, last >> (group - 1))
    pad = lambda x: jnp.concatenate([x, jnp.zeros((1, places - x.shape[1]), I32)], axis=1)
    src, payload, opens, last = order(slot_row, live, tile_row, tiles, slots, 2, places)
    rows = [src, payload, opens, pad(empty(last, 2, pairs_f))]
    src, payload, opens, last = order(tile_row, live, slot_row, slots, tiles, 2, places)
    rows += [src, payload, opens, pad(empty(last, 2, pairs_b))]
    src, _, opens, last = order(ray_row, every, ray_row, 0, rays, 1, 128)
    rows += [pad(src), pad(opens), pad(empty(last, 1, n_region))]
    for i, row in enumerate(rows):
        rows_v[i : i + 1, :] = row
    to_scalar = pltpu.make_async_copy(rows_v, rows_s, sem_rows)
    to_scalar.start()

    load_v.wait()
    for t in range(tiles):
        vol_b[t] = vol[t].astype(BF)
    vol_b[tiles] = jnp.zeros((size, size), BF)
    for c, m in enumerate(sizes):
        recv2[c][slots] = jnp.zeros((m, size), BF)
    runs_f[pairs_f] = jnp.zeros((most, size), BF)
    runs_b[pairs_b] = jnp.zeros((most, size), F32)
    runs_p[n_region] = jnp.zeros((most, size), F32)
    to_scalar.wait()
    for load in load_b:
        load.wait()

    def products(left, base, transposed, runs, pairs, unroll, m):
        def step(g, total):
            for u in range(unroll):
                p = g * unroll + u
                e0, e1 = rows_s[base, 2 * p], rows_s[base, 2 * p + 1]
                k0, k1 = rows_s[base + 1, 2 * p], rows_s[base + 1, 2 * p + 1]
                opened = rows_s[base + 2, 2 * p]
                lhs = jnp.concatenate([left[k0], left[k1]], axis=1)
                rhs = jnp.concatenate([blocks[e0], blocks[e1]], axis=1 if transposed else 0)
                dims = (((1,), (1,)), ((), ())) if transposed else (((1,), (0,)), ((), ()))
                product = lax.dot_general(lhs, rhs, dims, preferred_element_type=F32)
                total = jnp.where(opened > 0, 0.0, total) + product
                runs[p, pl.ds(0, m), :] = total.astype(runs.dtype)
            return total

        lax.fori_loop(0, pairs // unroll, step, jnp.zeros((m, size), F32))

    def exchange(src, dst, ssem, rsem, c):
        for peer in peers:
            pltpu.make_async_remote_copy(
                src_ref=src.at[peer, parts[c]], dst_ref=dst[c].at[r],
                send_sem=ssem.at[c], recv_sem=rsem.at[c], device_id=(peer, a), device_id_type=MESH,
            ).start()
        dst[c][r] = src[r, parts[c], :]

    def arrived(dst, sem, c):
        part = dst[c].at[pl.ds(0, n_region - 1)]
        pltpu.make_async_copy(part, part, sem.at[c]).wait()

    for c, m in enumerate(sizes):
        rows_at = parts[c]
        products(vol_b.at[:, rows_at], 0, True, runs_f, pairs_f, UNROLL_F, m)
        for s in range(slots):
            send1[s, rows_at, :] = runs_f[rows_s[3, s], pl.ds(0, m), :]
        if c == 0:
            pl.semaphore_wait(barrier, len(peers) + len(others))
        exchange(send1, recv1, ssem1, rsem1, c)

    load_s.wait()
    for c, m in enumerate(sizes):
        rows_at = parts[c]
        arrived(recv1, rsem1, c)
        total = jnp.zeros((m, size), F32)
        for k in range(n_region):
            total = jnp.where(rows_s[9, k] > 0, 0.0, total) + recv1[c][rows_s[8, k]].astype(F32)
            runs_p[k, pl.ds(0, m), :] = total
        for j in range(rays):
            value = rw_v[j : j + 1, :] * (sino[j, rows_at, :] - runs_p[rows_s[10, j], pl.ds(0, m), :])
            res[j, rows_at, :] = value
            res_b[j, rows_at, :] = value.astype(BF)
        for s in range(n_region):
            send2[s, rows_at, :] = res_b[ray_s[s], rows_at, :]
        exchange(send2, recv2, ssem2, rsem2, c)

    for c, m in enumerate(sizes):
        rows_at = parts[c]
        arrived(recv2, rsem2, c)
        products(recv2[c], 4, False, runs_b, pairs_b, UNROLL_B, m)
        for t in range(tiles):
            value = runs_b[rows_s[7, t], pl.ds(0, m), :]
            grad[t, rows_at, :] = value
            send3[c][t // share, t % share] = value.astype(BF)
        for other in others:
            pltpu.make_async_remote_copy(
                src_ref=send3[c].at[other], dst_ref=recv3[c].at[a],
                send_sem=ssem3.at[c], recv_sem=rsem3.at[c], device_id=(r, other), device_id_type=MESH,
            ).start()
        recv3[c][a] = jnp.zeros((share, m, size), BF)

    for c, m in enumerate(sizes):
        rows_at = parts[c]
        part = recv3[c].at[pl.ds(0, n_angle - 1)]
        pltpu.make_async_copy(part, part, rsem3.at[c]).wait()
        for t in range(share):
            mine = a * share + t
            total = grad[mine, rows_at, :]
            for k in range(n_angle):
                total = total + recv3[c][k, t].astype(F32)
            upd[t, rows_at, :] = vol[mine, rows_at, :] + pw_v[pl.ds(mine, 1), :] * total

    for c in range(chunks):
        for src, sem in ((send1, ssem1), (send2, ssem2)):
            part = src.at[pl.ds(0, n_region - 1), parts[c]]
            pltpu.make_async_copy(part, part, sem.at[c]).wait()
        part = send3[c].at[pl.ds(0, n_angle - 1)]
        pltpu.make_async_copy(part, part, ssem3.at[c]).wait()


def store_kernel(upd, res, updated_h, residual_h, sem):
    copies = [
        pltpu.make_async_copy(res, residual_h, sem.at[0]),
        pltpu.make_async_copy(upd, updated_h, sem.at[1]),
    ]
    for copy in copies:
        copy.start()
    for copy in copies:
        copy.wait()


def up(value, step):
    return -(-value // step) * step


def body(volume, blocks, tile_of, slot_of, live_count, ray_of, sinogram, ray_weight, pixel_weight):
    n_region = lax.axis_size("region")
    n_angle = lax.axis_size("angle")
    entries, size, _ = blocks.shape
    tiles, rays = volume.shape[0], sinogram.shape[0]
    sizes = SIZES
    chunks, most = len(sizes), max(sizes)
    share = tiles // n_angle
    pairs_f = up((entries + n_region) // 2, UNROLL_F)
    pairs_b = up((entries + tiles) // 2, UNROLL_B)
    places = up(2 * max(pairs_f, pairs_b), 128)
    smem = pl.BlockSpec(memory_space=pltpu.SMEM)
    vmem = pl.BlockSpec(memory_space=pltpu.VMEM)
    hbm = pl.BlockSpec(memory_space=pl.ANY)
    upd, res = pl.pallas_call(
        functools.partial(kernel, n_region, n_angle, sizes),
        out_shape=(
            pltpu.VMEM((share, size, size), F32),
            pltpu.VMEM((rays, size, size), F32),
        ),
        in_specs=[smem, smem, vmem, vmem, vmem, vmem, vmem, hbm, hbm, hbm],
        out_specs=(vmem, vmem),
        scratch_shapes=[
            pltpu.VMEM((entries, size, size), BF),
            pltpu.VMEM((tiles, size, size), F32),
            pltpu.VMEM((rays, size, size), F32),
            pltpu.VMEM((tiles + 1, size, size), BF),
            pltpu.VMEM((pairs_f + 1, most, size), BF),
            pltpu.VMEM((pairs_b + 1, most, size), F32),
            pltpu.VMEM((n_region + 1, most, size), F32),
            pltpu.VMEM((16, places), I32),
            pltpu.SMEM((16, places), I32),
            pltpu.VMEM((n_region, size, size), BF),
            [pltpu.VMEM((n_region, m, size), BF) for m in sizes],
            pltpu.VMEM((rays, size, size), BF),
            pltpu.VMEM((n_region, size, size), BF),
            [pltpu.VMEM((n_region + 1, m, size), BF) for m in sizes],
            pltpu.VMEM((tiles, size, size), F32),
            [pltpu.VMEM((n_angle, share, m, size), BF) for m in sizes],
            [pltpu.VMEM((n_angle, share, m, size), BF) for m in sizes],
            pltpu.SemaphoreType.DMA((2 + LOADS,)),
            pltpu.SemaphoreType.DMA,
        ]
        + [pltpu.SemaphoreType.DMA((chunks,))] * 6,
        compiler_params=pltpu.CompilerParams(
            collective_id=0, has_side_effects=True, vmem_limit_bytes=56 * 2**20
        ),
    )(
        live_count, ray_of, tile_of.reshape(1, entries), slot_of.reshape(1, entries), ray_of.reshape(1, n_region),
        ray_weight, pixel_weight, volume, blocks, sinogram,
    )
    return pl.pallas_call(
        store_kernel,
        out_shape=(
            jax.ShapeDtypeStruct((share, size, size), F32),
            jax.ShapeDtypeStruct((rays, size, size), F32),
        ),
        in_specs=[vmem, vmem],
        out_specs=(hbm, hbm),
        scratch_shapes=[pltpu.SemaphoreType.DMA((2,))],
        compiler_params=pltpu.CompilerParams(vmem_limit_bytes=2**20),
    )(upd, res)


def solution(mesh):
    placed = (
        P("region", None, None),
        P(("region", "angle"), None, None),
        P(("region", "angle")),
        P(("region", "angle")),
        P(("region", "angle")),
        P(("region", "angle")),
        P(("region", "angle"), None, None),
        P(("region", "angle"), None),
        P("region", None),
    )
    return jax.shard_map(
        body,
        mesh=mesh,
        in_specs=placed,
        out_specs=(P(("region", "angle"), None, None), P(("region", "angle"), None, None)),
        check_vma=False,
    )
```

```python
import functools

import jax
import jax.numpy as jnp
from jax import lax
from jax.experimental import pallas as pl
from jax.experimental.pallas import tpu as pltpu
from jax.sharding import PartitionSpec as P

MESH = pl.DeviceIdType.MESH
BF = jnp.bfloat16
F32 = jnp.float32
I32 = jnp.int32

SIZES = (32, 32, 32, 32)
UNROLL_F, UNROLL_B = 36, 34
LOADS = 4
NY = 4


def iota(shape, dim):
    return lax.broadcasted_iota(I32, shape, dim)


def order(key_row, live_row, payload_row, pad, keys, group, places):
    n = key_row.shape[1]
    row, col = iota((n, n), 0), iota((n, n), 1)
    key_row = jnp.where(live_row, key_row, keys)
    diag = row == col
    key_col = jnp.sum(jnp.where(diag, key_row, 0), axis=1, keepdims=True)
    payload_col = jnp.sum(jnp.where(diag, payload_row, 0), axis=1, keepdims=True)
    earlier = jnp.where((key_col == key_row) & (col < row), 1, 0)
    rank_col = jnp.sum(earlier, axis=1, keepdims=True)
    lane = iota((n, 128), 1)
    same = key_col == lane
    count_row = jnp.sum(jnp.where(same, 1, 0), axis=0, keepdims=True)
    run_row = (count_row + (group - 1)) & -group
    start_col = jnp.sum(jnp.where(lane < key_col, run_row, 0), axis=1, keepdims=True)
    place_col = jnp.where(key_col < keys, start_col + rank_col, 1 << 20)
    hit = place_col == iota((n, places), 1)
    entry = iota((n, places), 0)
    src = jnp.sum(jnp.where(hit, entry, 0), axis=0, keepdims=True)
    payload = jnp.sum(jnp.where(hit, payload_col - pad, 0), axis=0, keepdims=True) + pad
    opens = jnp.sum(jnp.where(hit & (rank_col == 0), 1, 0), axis=0, keepdims=True)
    last = jnp.max(jnp.where(same, place_col, -1), axis=0, keepdims=True)
    return src, payload, opens, last


def kernel(
    n_region, n_angle, sizes,
    count_s, ray_s, tile_v, slot_v, ray_v, rw_v, pw_v, volume_h, blocks_h, sino_h,
    upd, res,
    blocks, vol, sino, vol_b, runs_f, runs_b, runs_p, rows_v, rows_s,
    send1, recv1, res_b, send2, recv2, grad, send3, recv3,
    sem_in, sem_rows, ssem1, rsem1, ssem2, rsem2, ssem3, rsem3,
):
    r = lax.axis_index("region")
    a = lax.axis_index("angle")
    z, y = r // NY, lax.rem(r, NY)
    nz = n_region // NY
    entries = blocks.shape[0]
    tiles = vol.shape[0]
    slots = n_region
    rays = sino.shape[0]
    size = vol.shape[1]
    chunks = len(sizes)
    parts = [pl.ds(sum(sizes[:c]), m) for c, m in enumerate(sizes)]
    most = max(sizes)
    pairs_f = runs_f.shape[0] - 1
    pairs_b = runs_b.shape[0] - 1
    share = tiles // n_angle

    piece = entries // LOADS
    load_b = [
        pltpu.make_async_copy(blocks_h.at[pl.ds(i * piece, piece)], blocks.at[pl.ds(i * piece, piece)], sem_in.at[2 + i])
        for i in range(LOADS)
    ]
    load_v = pltpu.make_async_copy(volume_h, vol, sem_in.at[0])
    load_s = pltpu.make_async_copy(sino_h, sino, sem_in.at[1])
    load_v.start()
    for load in load_b:
        load.start()
    load_s.start()

    far = lambda d, n: min(d, n - d)
    steps = [(dz, dy) for dz in range(nz) for dy in range(NY) if (dz, dy) != (0, 0)]
    steps.sort(key=lambda o: -(far(o[0], nz) + far(o[1], NY)))
    peers = [lax.rem(z + dz, nz) * NY + lax.rem(y + dy, NY) for dz, dy in steps]
    others = [lax.rem(a + k, n_angle) for k in range(1, n_angle)]
    barrier = pltpu.get_barrier_semaphore()
    for peer in peers:
        pl.semaphore_signal(barrier, inc=1, device_id=(peer, a), device_id_type=MESH)
    for other in others:
        pl.semaphore_signal(barrier, inc=1, device_id=(r, other), device_id_type=MESH)

    live = lax.broadcasted_iota(I32, (1, entries), 1) < count_s[0]
    tile_row, slot_row = tile_v[...], slot_v[...]
    ray_row = jnp.concatenate([ray_v[...], jnp.zeros((1, 128 - n_region), I32)], axis=1)
    places = rows_v.shape[1]
    every = lax.broadcasted_iota(I32, ray_row.shape, 1) < n_region
    empty = lambda last, group, none: jnp.where(last < 0, none, last >> (group - 1))
    pad = lambda x: jnp.concatenate([x, jnp.zeros((1, places - x.shape[1]), I32)], axis=1)
    src, payload, opens, last = order(slot_row, live, tile_row, tiles, slots, 2, places)
    rows = [src, payload, opens, pad(empty(last, 2, pairs_f))]
    src, payload, opens, last = order(tile_row, live, slot_row, slots, tiles, 2, places)
    rows += [src, payload, opens, pad(empty(last, 2, pairs_b))]
    src, _, opens, last = order(ray_row, every, ray_row, 0, rays, 1, 128)
    rows += [pad(src), pad(opens), pad(empty(last, 1, n_region))]
    for i, row in enumerate(rows):
        rows_v[i : i + 1, :] = row
    to_scalar = pltpu.make_async_copy(rows_v, rows_s, sem_rows)
    to_scalar.start()

    load_v.wait()
    for t in range(tiles):
        vol_b[t] = vol[t].astype(BF)
    vol_b[tiles] = jnp.zeros((size, size), BF)
    for c, m in enumerate(sizes):
        recv2[c][slots] = jnp.zeros((m, size), BF)
    runs_f[pairs_f] = jnp.zeros((most, size), BF)
    runs_b[pairs_b] = jnp.zeros((most, size), F32)
    runs_p[n_region] = jnp.zeros((most, size), F32)
    to_scalar.wait()
    for load in load_b:
        load.wait()

    def products(left, base, transposed, runs, pairs, unroll, m):
        def step(g, total):
            for u in range(unroll):
                p = g * unroll + u
                e0, e1 = rows_s[base, 2 * p], rows_s[base, 2 * p + 1]
                k0, k1 = rows_s[base + 1, 2 * p], rows_s[base + 1, 2 * p + 1]
                opened = rows_s[base + 2, 2 * p]
                lhs = jnp.concatenate([left[k0], left[k1]], axis=1)
                rhs = jnp.concatenate([blocks[e0], blocks[e1]], axis=1 if transposed else 0)
                dims = (((1,), (1,)), ((), ())) if transposed else (((1,), (0,)), ((), ()))
                product = lax.dot_general(lhs, rhs, dims, preferred_element_type=F32)
                total = jnp.where(opened > 0, 0.0, total) + product
                runs[p, pl.ds(0, m), :] = total.astype(runs.dtype)
            return total

        lax.fori_loop(0, pairs // unroll, step, jnp.zeros((m, size), F32))

    def exchange(src, dst, ssem, rsem, c):
        for peer in peers:
            pltpu.make_async_remote_copy(
                src_ref=src.at[peer, parts[c]], dst_ref=dst[c].at[r],
                send_sem=ssem.at[c], recv_sem=rsem.at[c], device_id=(peer, a), device_id_type=MESH,
            ).start()
        dst[c][r] = src[r, parts[c], :]

    def arrived(dst, sem, c):
        part = dst[c].at[pl.ds(0, n_region - 1)]
        pltpu.make_async_copy(part, part, sem.at[c]).wait()

    for c, m in enumerate(sizes):
        rows_at = parts[c]
        products(vol_b.at[:, rows_at], 0, True, runs_f, pairs_f, UNROLL_F, m)
        for s in range(slots):
            send1[s, rows_at, :] = runs_f[rows_s[3, s], pl.ds(0, m), :]
        if c == 0:
            pl.semaphore_wait(barrier, len(peers) + len(others))
        exchange(send1, recv1, ssem1, rsem1, c)

    load_s.wait()
    for c, m in enumerate(sizes):
        rows_at = parts[c]
        arrived(recv1, rsem1, c)
        total = jnp.zeros((m, size), F32)
        for k in range(n_region):
            total = jnp.where(rows_s[9, k] > 0, 0.0, total) + recv1[c][rows_s[8, k]].astype(F32)
            runs_p[k, pl.ds(0, m), :] = total
        for j in range(rays):
            value = rw_v[j : j + 1, :] * (sino[j, rows_at, :] - runs_p[rows_s[10, j], pl.ds(0, m), :])
            res[j, rows_at, :] = value
            res_b[j, rows_at, :] = value.astype(BF)
        for s in range(n_region):
            send2[s, rows_at, :] = res_b[ray_s[s], rows_at, :]
        exchange(send2, recv2, ssem2, rsem2, c)

    for c, m in enumerate(sizes):
        rows_at = parts[c]
        arrived(recv2, rsem2, c)
        products(recv2[c], 4, False, runs_b, pairs_b, UNROLL_B, m)
        for t in range(tiles):
            value = runs_b[rows_s[7, t], pl.ds(0, m), :]
            grad[t, rows_at, :] = value
            send3[c][t // share, t % share] = value.astype(BF)
        for other in others:
            pltpu.make_async_remote_copy(
                src_ref=send3[c].at[other], dst_ref=recv3[c].at[a],
                send_sem=ssem3.at[c], recv_sem=rsem3.at[c], device_id=(r, other), device_id_type=MESH,
            ).start()
        recv3[c][a] = jnp.zeros((share, m, size), BF)

    for c, m in enumerate(sizes):
        rows_at = parts[c]
        part = recv3[c].at[pl.ds(0, n_angle - 1)]
        pltpu.make_async_copy(part, part, rsem3.at[c]).wait()
        for t in range(share):
            mine = a * share + t
            total = grad[mine, rows_at, :]
            for k in range(n_angle):
                total = total + recv3[c][k, t].astype(F32)
            upd[t, rows_at, :] = vol[mine, rows_at, :] + pw_v[pl.ds(mine, 1), :] * total

    for c in range(chunks):
        for src, sem in ((send1, ssem1), (send2, ssem2)):
            part = src.at[pl.ds(0, n_region - 1), parts[c]]
            pltpu.make_async_copy(part, part, sem.at[c]).wait()
        part = send3[c].at[pl.ds(0, n_angle - 1)]
        pltpu.make_async_copy(part, part, ssem3.at[c]).wait()


def store_kernel(upd, res, updated_h, residual_h, sem):
    copies = [
        pltpu.make_async_copy(res, residual_h, sem.at[0]),
        pltpu.make_async_copy(upd, updated_h, sem.at[1]),
    ]
    for copy in copies:
        copy.start()
    for copy in copies:
        copy.wait()


def up(value, step):
    return -(-value // step) * step


def body(volume, blocks, tile_of, slot_of, live_count, ray_of, sinogram, ray_weight, pixel_weight):
    n_region = lax.axis_size("region")
    n_angle = lax.axis_size("angle")
    entries, size, _ = blocks.shape
    tiles, rays = volume.shape[0], sinogram.shape[0]
    sizes = SIZES
    chunks, most = len(sizes), max(sizes)
    share = tiles // n_angle
    pairs_f = up((entries + n_region) // 2, UNROLL_F)
    pairs_b = up((entries + tiles) // 2, UNROLL_B)
    places = up(2 * max(pairs_f, pairs_b), 128)
    smem = pl.BlockSpec(memory_space=pltpu.SMEM)
    vmem = pl.BlockSpec(memory_space=pltpu.VMEM)
    hbm = pl.BlockSpec(memory_space=pl.ANY)
    upd, res = pl.pallas_call(
        functools.partial(kernel, n_region, n_angle, sizes),
        out_shape=(
            pltpu.VMEM((share, size, size), F32),
            pltpu.VMEM((rays, size, size), F32),
        ),
        in_specs=[smem, smem, vmem, vmem, vmem, vmem, vmem, hbm, hbm, hbm],
        out_specs=(vmem, vmem),
        scratch_shapes=[
            pltpu.VMEM((entries, size, size), BF),
            pltpu.VMEM((tiles, size, size), F32),
            pltpu.VMEM((rays, size, size), F32),
            pltpu.VMEM((tiles + 1, size, size), BF),
            pltpu.VMEM((pairs_f + 1, most, size), BF),
            pltpu.VMEM((pairs_b + 1, most, size), F32),
            pltpu.VMEM((n_region + 1, most, size), F32),
            pltpu.VMEM((16, places), I32),
            pltpu.SMEM((16, places), I32),
            pltpu.VMEM((n_region, size, size), BF),
            [pltpu.VMEM((n_region, m, size), BF) for m in sizes],
            pltpu.VMEM((rays, size, size), BF),
            pltpu.VMEM((n_region, size, size), BF),
            [pltpu.VMEM((n_region + 1, m, size), BF) for m in sizes],
            pltpu.VMEM((tiles, size, size), F32),
            [pltpu.VMEM((n_angle, share, m, size), BF) for m in sizes],
            [pltpu.VMEM((n_angle, share, m, size), BF) for m in sizes],
            pltpu.SemaphoreType.DMA((2 + LOADS,)),
            pltpu.SemaphoreType.DMA,
        ]
        + [pltpu.SemaphoreType.DMA((chunks,))] * 6,
        compiler_params=pltpu.CompilerParams(
            collective_id=0, has_side_effects=True, vmem_limit_bytes=56 * 2**20
        ),
    )(
        live_count, ray_of, tile_of.reshape(1, entries), slot_of.reshape(1, entries), ray_of.reshape(1, n_region),
        ray_weight, pixel_weight, volume, blocks, sinogram,
    )
    return pl.pallas_call(
        store_kernel,
        out_shape=(
            jax.ShapeDtypeStruct((share, size, size), F32),
            jax.ShapeDtypeStruct((rays, size, size), F32),
        ),
        in_specs=[vmem, vmem],
        out_specs=(hbm, hbm),
        scratch_shapes=[pltpu.SemaphoreType.DMA((2,))],
        compiler_params=pltpu.CompilerParams(vmem_limit_bytes=2**20),
    )(upd, res)


def solution(mesh):
    placed = (
        P("region", None, None),
        P(("region", "angle"), None, None),
        P(("region", "angle")),
        P(("region", "angle")),
        P(("region", "angle")),
        P(("region", "angle")),
        P(("region", "angle"), None, None),
        P(("region", "angle"), None),
        P("region", None),
    )
    return jax.shard_map(
        body,
        mesh=mesh,
        in_specs=placed,
        out_specs=(P(("region", "angle"), None, None), P(("region", "angle"), None, None)),
        check_vma=False,
    )
```

```python
import functools

import jax
import jax.numpy as jnp
from jax import lax
from jax.experimental import pallas as pl
from jax.experimental.pallas import tpu as pltpu
from jax.sharding import PartitionSpec as P

MESH = pl.DeviceIdType.MESH
BF = jnp.bfloat16
F32 = jnp.float32
I32 = jnp.int32

SIZES = (32, 32, 32, 32)
UNROLL_F, UNROLL_B = 36, 34
LOADS = 4
NY = 4


def iota(shape, dim):
    return lax.broadcasted_iota(I32, shape, dim)


def order(key_row, live_row, payload_row, pad, keys, group, places):
    n = key_row.shape[1]
    row, col = iota((n, n), 0), iota((n, n), 1)
    key_row = jnp.where(live_row, key_row, keys)
    diag = row == col
    key_col = jnp.sum(jnp.where(diag, key_row, 0), axis=1, keepdims=True)
    payload_col = jnp.sum(jnp.where(diag, payload_row, 0), axis=1, keepdims=True)
    earlier = jnp.where((key_col == key_row) & (col < row), 1, 0)
    rank_col = jnp.sum(earlier, axis=1, keepdims=True)
    lane = iota((n, 128), 1)
    same = key_col == lane
    count_row = jnp.sum(jnp.where(same, 1, 0), axis=0, keepdims=True)
    run_row = (count_row + (group - 1)) & -group
    start_col = jnp.sum(jnp.where(lane < key_col, run_row, 0), axis=1, keepdims=True)
    place_col = jnp.where(key_col < keys, start_col + rank_col, 1 << 20)
    hit = place_col == iota((n, places), 1)
    entry = iota((n, places), 0)
    src = jnp.sum(jnp.where(hit, entry, 0), axis=0, keepdims=True)
    payload = jnp.sum(jnp.where(hit, payload_col - pad, 0), axis=0, keepdims=True) + pad
    opens = jnp.sum(jnp.where(hit & (rank_col == 0), 1, 0), axis=0, keepdims=True)
    last = jnp.max(jnp.where(same, place_col, -1), axis=0, keepdims=True)
    return src, payload, opens, last


def kernel(
    n_region, n_angle, sizes,
    count_s, ray_s, tile_v, slot_v, ray_v, rw_v, pw_v, volume_h, blocks_h, sino_h,
    upd, res,
    blocks, vol, sino, vol_b, runs_f, runs_b, runs_p, rows_v, rows_s,
    send1, recv1, res_b, send2, recv2, grad, send3, recv3,
    sem_in, sem_rows, ssem1, rsem1, ssem2, rsem2, ssem3, rsem3,
):
    r = lax.axis_index("region")
    a = lax.axis_index("angle")
    z, y = r // NY, lax.rem(r, NY)
    nz = n_region // NY
    entries = blocks.shape[0]
    tiles = vol.shape[0]
    slots = n_region
    rays = sino.shape[0]
    size = vol.shape[1]
    chunks = len(sizes)
    parts = [pl.ds(sum(sizes[:c]), m) for c, m in enumerate(sizes)]
    most = max(sizes)
    pairs_f = runs_f.shape[0] - 1
    pairs_b = runs_b.shape[0] - 1
    share = tiles // n_angle

    piece = entries // LOADS
    load_b = [
        pltpu.make_async_copy(blocks_h.at[pl.ds(i * piece, piece)], blocks.at[pl.ds(i * piece, piece)], sem_in.at[2 + i])
        for i in range(LOADS)
    ]
    load_v = pltpu.make_async_copy(volume_h, vol, sem_in.at[0])
    load_s = pltpu.make_async_copy(sino_h, sino, sem_in.at[1])
    load_v.start()
    for load in load_b:
        load.start()
    load_s.start()

    far = lambda d, n: min(d, n - d)
    steps = [(dz, dy) for dz in range(nz) for dy in range(NY) if (dz, dy) != (0, 0)]
    steps.sort(key=lambda o: -(far(o[0], nz) + far(o[1], NY)))
    peers = [lax.rem(z + dz, nz) * NY + lax.rem(y + dy, NY) for dz, dy in steps]
    others = [lax.rem(a + k, n_angle) for k in range(1, n_angle)]
    barrier = pltpu.get_barrier_semaphore()
    for peer in peers:
        pl.semaphore_signal(barrier, inc=1, device_id=(peer, a), device_id_type=MESH)
    for other in others:
        pl.semaphore_signal(barrier, inc=1, device_id=(r, other), device_id_type=MESH)

    live = lax.broadcasted_iota(I32, (1, entries), 1) < count_s[0]
    tile_row, slot_row = tile_v[...], slot_v[...]
    ray_row = jnp.concatenate([ray_v[...], jnp.zeros((1, 128 - n_region), I32)], axis=1)
    places = rows_v.shape[1]
    every = lax.broadcasted_iota(I32, ray_row.shape, 1) < n_region
    empty = lambda last, group, none: jnp.where(last < 0, none, last >> (group - 1))
    pad = lambda x: jnp.concatenate([x, jnp.zeros((1, places - x.shape[1]), I32)], axis=1)
    src, payload, opens, last = order(slot_row, live, tile_row, tiles, slots, 2, places)
    rows = [src, payload, opens, pad(empty(last, 2, pairs_f))]
    src, payload, opens, last = order(tile_row, live, slot_row, slots, tiles, 2, places)
    rows += [src, payload, opens, pad(empty(last, 2, pairs_b))]
    src, _, opens, last = order(ray_row, every, ray_row, 0, rays, 1, 128)
    rows += [pad(src), pad(opens), pad(empty(last, 1, n_region))]
    for i, row in enumerate(rows):
        rows_v[i : i + 1, :] = row
    to_scalar = pltpu.make_async_copy(rows_v, rows_s, sem_rows)
    to_scalar.start()

    load_v.wait()
    for t in range(tiles):
        vol_b[t] = vol[t].astype(BF)
    vol_b[tiles] = jnp.zeros((size, size), BF)
    for c, m in enumerate(sizes):
        recv2[c][slots] = jnp.zeros((m, size), BF)
    runs_f[pairs_f] = jnp.zeros((most, size), BF)
    runs_b[pairs_b] = jnp.zeros((most, size), F32)
    runs_p[n_region] = jnp.zeros((most, size), F32)
    to_scalar.wait()
    for load in load_b:
        load.wait()

    def products(left, base, transposed, runs, pairs, unroll, m):
        def step(g, total):
            for u in range(unroll):
                p = g * unroll + u
                e0, e1 = rows_s[base, 2 * p], rows_s[base, 2 * p + 1]
                k0, k1 = rows_s[base + 1, 2 * p], rows_s[base + 1, 2 * p + 1]
                opened = rows_s[base + 2, 2 * p]
                lhs = jnp.concatenate([left[k0], left[k1]], axis=1)
                rhs = jnp.concatenate([blocks[e0], blocks[e1]], axis=1 if transposed else 0)
                dims = (((1,), (1,)), ((), ())) if transposed else (((1,), (0,)), ((), ()))
                product = lax.dot_general(lhs, rhs, dims, preferred_element_type=F32)
                total = jnp.where(opened > 0, 0.0, total) + product
                runs[p, pl.ds(0, m), :] = total.astype(runs.dtype)
            return total

        lax.fori_loop(0, pairs // unroll, step, jnp.zeros((m, size), F32))

    def exchange(src, dst, ssem, rsem, c):
        for peer in peers:
            pltpu.make_async_remote_copy(
                src_ref=src.at[peer, parts[c]], dst_ref=dst[c].at[r],
                send_sem=ssem.at[c], recv_sem=rsem.at[c], device_id=(peer, a), device_id_type=MESH,
            ).start()
        dst[c][r] = src[r, parts[c], :]

    def arrived(dst, sem, c):
        part = dst[c].at[pl.ds(0, n_region - 1)]
        pltpu.make_async_copy(part, part, sem.at[c]).wait()

    for c, m in enumerate(sizes):
        rows_at = parts[c]
        products(vol_b.at[:, rows_at], 0, True, runs_f, pairs_f, UNROLL_F, m)
        for s in range(slots):
            send1[s, rows_at, :] = runs_f[rows_s[3, s], pl.ds(0, m), :]
        if c == 0:
            pl.semaphore_wait(barrier, len(peers) + len(others))
        exchange(send1, recv1, ssem1, rsem1, c)

    load_s.wait()
    for c, m in enumerate(sizes):
        rows_at = parts[c]
        arrived(recv1, rsem1, c)
        total = jnp.zeros((m, size), F32)
        for k in range(n_region):
            total = jnp.where(rows_s[9, k] > 0, 0.0, total) + recv1[c][rows_s[8, k]].astype(F32)
            runs_p[k, pl.ds(0, m), :] = total
        for j in range(rays):
            value = rw_v[j : j + 1, :] * (sino[j, rows_at, :] - runs_p[rows_s[10, j], pl.ds(0, m), :])
            res[j, rows_at, :] = value
            res_b[j, rows_at, :] = value.astype(BF)
        for s in range(n_region):
            send2[s, rows_at, :] = res_b[ray_s[s], rows_at, :]
        exchange(send2, recv2, ssem2, rsem2, c)

    def finish(c):
        rows_at = parts[c]
        part = recv3[c].at[pl.ds(0, n_angle - 1)]
        pltpu.make_async_copy(part, part, rsem3.at[c]).wait()
        for t in range(share):
            mine = a * share + t
            total = grad[mine, rows_at, :]
            for k in range(n_angle):
                total = total + recv3[c][k, t].astype(F32)
            upd[t, rows_at, :] = vol[mine, rows_at, :] + pw_v[pl.ds(mine, 1), :] * total

    for c, m in enumerate(sizes):
        rows_at = parts[c]
        arrived(recv2, rsem2, c)
        products(recv2[c], 4, False, runs_b, pairs_b, UNROLL_B, m)
        for t in range(tiles):
            value = runs_b[rows_s[7, t], pl.ds(0, m), :]
            grad[t, rows_at, :] = value
            send3[c][t // share, t % share] = value.astype(BF)
        for other in others:
            pltpu.make_async_remote_copy(
                src_ref=send3[c].at[other], dst_ref=recv3[c].at[a],
                send_sem=ssem3.at[c], recv_sem=rsem3.at[c], device_id=(r, other), device_id_type=MESH,
            ).start()
        recv3[c][a] = jnp.zeros((share, m, size), BF)
        if c:
            finish(c - 1)
    finish(chunks - 1)

    for c in range(chunks):
        for src, sem in ((send1, ssem1), (send2, ssem2)):
            part = src.at[pl.ds(0, n_region - 1), parts[c]]
            pltpu.make_async_copy(part, part, sem.at[c]).wait()
        part = send3[c].at[pl.ds(0, n_angle - 1)]
        pltpu.make_async_copy(part, part, ssem3.at[c]).wait()


def store_kernel(upd, res, updated_h, residual_h, sem):
    copies = [pltpu.make_async_copy(upd, updated_h, sem.at[0])]
    for j in range(4):
        part = pl.ds(2 * j, 2)
        copies.append(pltpu.make_async_copy(res.at[part], residual_h.at[part], sem.at[1 + j]))
    for copy in copies:
        copy.start()
    for copy in copies:
        copy.wait()


def up(value, step):
    return -(-value // step) * step


def body(volume, blocks, tile_of, slot_of, live_count, ray_of, sinogram, ray_weight, pixel_weight):
    n_region = lax.axis_size("region")
    n_angle = lax.axis_size("angle")
    entries, size, _ = blocks.shape
    tiles, rays = volume.shape[0], sinogram.shape[0]
    sizes = SIZES
    chunks, most = len(sizes), max(sizes)
    share = tiles // n_angle
    pairs_f = up((entries + n_region) // 2, UNROLL_F)
    pairs_b = up((entries + tiles) // 2, UNROLL_B)
    places = up(2 * max(pairs_f, pairs_b), 128)
    smem = pl.BlockSpec(memory_space=pltpu.SMEM)
    vmem = pl.BlockSpec(memory_space=pltpu.VMEM)
    hbm = pl.BlockSpec(memory_space=pl.ANY)
    upd, res = pl.pallas_call(
        functools.partial(kernel, n_region, n_angle, sizes),
        out_shape=(
            pltpu.VMEM((share, size, size), F32),
            pltpu.VMEM((rays, size, size), F32),
        ),
        in_specs=[smem, smem, vmem, vmem, vmem, vmem, vmem, hbm, hbm, hbm],
        out_specs=(vmem, vmem),
        scratch_shapes=[
            pltpu.VMEM((entries, size, size), BF),
            pltpu.VMEM((tiles, size, size), F32),
            pltpu.VMEM((rays, size, size), F32),
            pltpu.VMEM((tiles + 1, size, size), BF),
            pltpu.VMEM((pairs_f + 1, most, size), BF),
            pltpu.VMEM((pairs_b + 1, most, size), F32),
            pltpu.VMEM((n_region + 1, most, size), F32),
            pltpu.VMEM((16, places), I32),
            pltpu.SMEM((16, places), I32),
            pltpu.VMEM((n_region, size, size), BF),
            [pltpu.VMEM((n_region, m, size), BF) for m in sizes],
            pltpu.VMEM((rays, size, size), BF),
            pltpu.VMEM((n_region, size, size), BF),
            [pltpu.VMEM((n_region + 1, m, size), BF) for m in sizes],
            pltpu.VMEM((tiles, size, size), F32),
            [pltpu.VMEM((n_angle, share, m, size), BF) for m in sizes],
            [pltpu.VMEM((n_angle, share, m, size), BF) for m in sizes],
            pltpu.SemaphoreType.DMA((2 + LOADS,)),
            pltpu.SemaphoreType.DMA,
        ]
        + [pltpu.SemaphoreType.DMA((chunks,))] * 6,
        compiler_params=pltpu.CompilerParams(
            collective_id=0, has_side_effects=True, vmem_limit_bytes=56 * 2**20
        ),
    )(
        live_count, ray_of, tile_of.reshape(1, entries), slot_of.reshape(1, entries), ray_of.reshape(1, n_region),
        ray_weight, pixel_weight, volume, blocks, sinogram,
    )
    return pl.pallas_call(
        store_kernel,
        out_shape=(
            jax.ShapeDtypeStruct((share, size, size), F32),
            jax.ShapeDtypeStruct((rays, size, size), F32),
        ),
        in_specs=[vmem, vmem],
        out_specs=(hbm, hbm),
        scratch_shapes=[pltpu.SemaphoreType.DMA((5,))],
        compiler_params=pltpu.CompilerParams(vmem_limit_bytes=2**20),
    )(upd, res)


def solution(mesh):
    placed = (
        P("region", None, None),
        P(("region", "angle"), None, None),
        P(("region", "angle")),
        P(("region", "angle")),
        P(("region", "angle")),
        P(("region", "angle")),
        P(("region", "angle"), None, None),
        P(("region", "angle"), None),
        P("region", None),
    )
    return jax.shard_map(
        body,
        mesh=mesh,
        in_specs=placed,
        out_specs=(P(("region", "angle"), None, None), P(("region", "angle"), None, None)),
        check_vma=False,
    )
```
